32 devices in a mesh: groups: 2 (over y), tile: 4 (over z), depth: 4 (over x, core).
Axes of the slice: x: 2, y: 2, z: 4, core: 2. Of those that a mesh axis runs over, the one named last changes fastest.
Arguments:
- volume: bfloat16 [64, 64, 32, 128], P(None, ('groups', 'depth'), 'tile'), parts along dimension 1, may hold values from -6 to 6
- first_kernel: bfloat16 [27, 64, 64], replicated, may hold values from -0.15625 to 0.15625
- first_bias: float32 [64], replicated, may hold values from -3 to 3
- second_kernel: bfloat16 [27, 64, 64], replicated, may hold values from -0.15625 to 0.15625
- second_bias: float32 [64], replicated, may hold values from -3 to 3
- density_weight: bfloat16 [64], replicated, may hold values from -0.75 to 0.75
Outputs:
- image: float32 [64, 64, 128], P('depth', ('groups', 'tile')), parts along dimension 1
The draws below stay inside these ranges and needn't reach their ends.
There are 2 independent parts, one for each index of `groups`. The reference program is written for one: setup_inputs(seed, part) draws one part's arguments, and reference() takes and returns one part's arrays. A program takes and returns all parts, laid end to end along the dimension named above; an argument that names none is the same for every part. Nothing has to cross between parts.
All inputs are finite; a program needn't handle non-finite values.
Results may differ from the reference program's by a relative error of at most 0.0015.
Values may be sent and summed in bfloat16 or wider, within the bound.
No kernel may reach another device: no remote copies, remote signals or barrier semaphores. Data moves between devices by JAX's collectives and lax.ppermute only.
A program may use at most 192 MiB of HBM per device.

```python
import jax
import jax.numpy as jnp
from jax import lax

C = 64
CY = 128
CZ = 8
NX = 32
NZ = 32
N_DEPTH = 4


def block_levels(key, shape, split, smallest, high):
    def one(dim, blocks):
        heights = jax.random.uniform(jax.random.fold_in(jax.random.fold_in(key, 6), dim), (blocks,), jnp.float32, smallest / len(split), high / len(split))
        return jnp.repeat(jnp.exp(heights), shape[dim] // blocks).reshape((-1,) + (1,) * (len(shape) - dim - 1))

    factor_of = one(*split[0])
    for cut in split[1:]:
        factor_of = factor_of * one(*cut)
    return factor_of


def scatter_about(own_key, dims, width, limit, split=(), kind=jnp.bfloat16):
    level = block_levels(own_key, dims, split, -0.22, 0.18) if split else 1.0
    entries = jax.random.normal(own_key, dims, jnp.float32) * width * level
    return jnp.minimum(jnp.maximum(entries, -limit), limit).astype(kind)


def setup_inputs(seed: int = 0, part: int = 0) -> dict:
    streams_of = jax.random.split(jax.random.key(seed), 7)
    part_splits = jax.random.split(jax.random.fold_in(streams_of[6], part), 7)
    volume = scatter_about(part_splits[0], (C, NZ, NX, CY), 1.0, 6.0, ((1, 4), (2, 4)))
    first_kernel = scatter_about(streams_of[1], (27, C, C), (27 * C) ** -0.5, 0.15625)
    first_bias = scatter_about(streams_of[2], (C,), 0.5, 3.0, (), jnp.float32)
    second_kernel = scatter_about(streams_of[3], (27, C, C), (27 * C) ** -0.5, 0.15625)
    second_bias = scatter_about(streams_of[4], (C,), 0.5, 3.0, (), jnp.float32)
    density_weight = scatter_about(streams_of[5], (C,), C ** -0.5, 0.75)
    return dict(volume=volume, first_kernel=first_kernel, first_bias=first_bias, second_kernel=second_kernel, second_bias=second_bias, density_weight=density_weight)


def convolve(field, kernel, bias, spacing):
    taps = kernel.reshape(3, 3, 3, C, C).transpose(3, 4, 0, 1, 2)
    out = lax.conv_general_dilated(field[None], taps, (1, 1, 1), [(spacing, spacing)] * 3, rhs_dilation=(spacing, spacing, spacing), dimension_numbers=("NCDHW", "OIDHW", "NCDHW"), preferred_element_type=jnp.float32)[0]
    return jax.nn.silu(out + bias[:, None, None, None]).astype(jnp.bfloat16)


def reference(volume, first_kernel, first_bias, second_kernel, second_bias, density_weight):
    hidden = convolve(volume, first_kernel, first_bias, 1)
    features = convolve(hidden, second_kernel, second_bias, 2)
    logits = jnp.einsum("c,czxy->zxy", density_weight, features, preferred_element_type=jnp.float32)
    tau = jax.nn.softplus(logits) * (2.0 / NZ)
    tau = tau.reshape(N_DEPTH, CZ, NX, CY)
    inner = jnp.cumsum(tau, axis=1) - tau
    ray_weight = (jnp.exp(-inner) * (-jnp.expm1(-tau))).astype(jnp.bfloat16)
    feats = features.reshape(C, N_DEPTH, CZ, NX, CY)
    slab_image = jnp.einsum("szxy,cszxy->scxy", ray_weight.astype(jnp.float32), feats.astype(jnp.float32))
    slab_depth = jnp.sum(tau, axis=1)
    prior = jnp.cumsum(slab_depth, axis=0) - slab_depth
    return jnp.sum(jnp.exp(-prior)[:, None] * slab_image, axis=0)
```

```python
import functools

import jax
import jax.numpy as jnp
from jax import lax
from jax.experimental import pallas as pl
from jax.experimental.pallas import tpu as pltpu
from jax.sharding import PartitionSpec as P

BF16 = jnp.bfloat16
F32 = jnp.float32
HALO = 3
VMEM = pl.BlockSpec(memory_space=pltpu.VMEM)


def near_pairs(count):
    return [(i, i ^ 1) for i in range(count) if i ^ 1 < count]


def far_pairs(count):
    lows = [i for i in range(1, count - 1, 2)]
    return [(i, i + 1) for i in lows] + [(i + 1, i) for i in lows]


def swap_edges(block, axis, dim, width):
    index, count = lax.axis_index(axis), lax.axis_size(axis)
    last = block.shape[dim] - width
    even = index % 2 == 0
    near = lax.dynamic_slice_in_dim(block, jnp.where(even, last, 0), width, dim)
    far = lax.dynamic_slice_in_dim(block, jnp.where(even, 0, last), width, dim)
    return (
        lax.ppermute(near, axis, near_pairs(count)),
        lax.ppermute(far, axis, far_pairs(count)),
    )


def shifted_sum(parts, spacing, chans):
    lanes = parts.shape[1]
    column = lax.broadcasted_iota(jnp.int32, (chans, lanes), 1)
    low = pltpu.roll(parts[:chans], spacing, 1)
    high = pltpu.roll(parts[2 * chans :], lanes - spacing, 1)
    return (
        parts[chans : 2 * chans]
        + jnp.where(column >= spacing, low, 0.0)
        + jnp.where(column < lanes - spacing, high, 0.0)
    )


def silu(value):
    half = 0.5 * value
    return half + half * jnp.tanh(half)


def column_of(row_ref, lanes):
    chans = row_ref.shape[1]
    return jnp.broadcast_to(row_ref[...].astype(F32), (lanes, chans)).T


def pack_taps(source_ref, packed_ref):
    chans_out, chans_in = source_ref.shape[1:]
    for tap in range(9):
        packed_ref[:, tap * chans_in : (tap + 1) * chans_in] = source_ref[3 * tap : 3 * tap + 3].reshape(
            3 * chans_out, chans_in
        )


def conv_spots(taps_ref, fetch, spots, spacing, chans, lanes):
    blocks = []
    for dz in range(3):
        for dx in range(3):
            blocks.append(
                jnp.concatenate([fetch(z + spacing * dz, x + spacing * dx) for z, x in spots], axis=1)
            )
    stacked = jnp.concatenate(blocks, axis=0)
    parts = jnp.dot(taps_ref[...], stacked, preferred_element_type=F32)
    return [shifted_sum(parts[:, r * lanes : (r + 1) * lanes], spacing, chans) for r in range(len(spots))]


def edge_list(length):
    return [0, 1, 2, length + 1, length + 2, length + 3]


def inner_kernel(own_ref, w1_ref, b1_ref, w2_ref, hidden_ref, taps1_ref, taps2_ref):
    planes, rows, chans, lanes = own_ref.shape
    pack_taps(w1_ref, taps1_ref)
    bias = column_of(b1_ref, lanes)

    def step(plane, carry):
        for x in range(HALO, rows + 1, 2):
            spots = [(plane, x), (plane, x + 1)]
            sums = conv_spots(taps1_ref, lambda z, x: own_ref[z - HALO, x - HALO], spots, 1, chans, lanes)
            for (z, x), value in zip(spots, sums):
                hidden_ref[z, x] = silu(value + bias).astype(BF16)
        return carry

    lax.fori_loop(HALO, planes + 1, step, 0)
    pack_taps(w2_ref, taps2_ref)


def side_kernel(own_ref, tiles_ref, depths_ref, taps_ref, b1_ref, given_ref, hidden_ref):
    planes, rows, chans, lanes = own_ref.shape
    tile_odd, depth_odd = lax.axis_index("tile") % 2, lax.axis_index("depth") % 2
    bias = column_of(b1_ref, lanes)

    def fetch_x(z, x):
        if x < HALO:
            return tiles_ref[1 - tile_odd, z - HALO, x]
        if x >= rows + HALO:
            return tiles_ref[tile_odd, z - HALO, x - HALO - rows]
        return own_ref[z - HALO, x - HALO]

    def fetch_z(z, x):
        if z < HALO:
            return depths_ref[1 - depth_odd, z, x - HALO]
        if z >= planes + HALO:
            return depths_ref[depth_odd, z - HALO - planes, x - HALO]
        return own_ref[z - HALO, x - HALO]

    def emit(spots, fetch):
        sums = conv_spots(taps_ref, fetch, spots, 1, chans, lanes)
        for (z, x), value in zip(spots, sums):
            hidden_ref[z, x] = silu(value + bias).astype(BF16)

    edge_x, edge_z = edge_list(rows), edge_list(planes)

    def step_x(plane, carry):
        for i in range(0, len(edge_x), 2):
            emit([(plane, edge_x[i]), (plane, edge_x[i + 1])], fetch_x)
        return carry

    def step_z(pair, carry):
        x = HALO + 2 * pair
        for z in edge_z:
            emit([(z, x), (z, x + 1)], fetch_z)
        return carry

    lax.fori_loop(0, (rows - 2) // 2, step_z, 0)
    lax.fori_loop(HALO, planes + 1, step_x, 0)


def split_groups(value, bit, unit):
    groups = [value[i : i + unit] for i in range(0, value.shape[0], unit)]
    even, odd = jnp.concatenate(groups[0::2], axis=0), jnp.concatenate(groups[1::2], axis=0)
    return jnp.where(bit == 1, even, odd), jnp.where(bit == 1, odd, even)


def put_image(row, rows, image, depth, bit, unit, send_ref, keep_ref):
    send, keep = split_groups(image, bit, unit)
    width = send_ref.shape[1]
    for ref, value in ((send_ref, send), (keep_ref, keep)):
        ref[row] = value
        ref[rows + row // width, pl.ds(row % width, 1)] = depth


def field_kernel(
    tau_scale,
    unit,
    own_ref,
    tiles_ref,
    depths_ref,
    corners_ref,
    taps1_ref,
    b1_ref,
    taps2_ref,
    b2_ref,
    dens_ref,
    given_ref,
    hidden_ref,
    send_ref,
    keep_ref,
):
    planes, rows, chans, lanes = own_ref.shape
    tile_index, depth_index = lax.axis_index("tile"), lax.axis_index("depth")
    tile_odd, depth_odd = tile_index % 2, depth_index % 2
    bias1 = column_of(b1_ref, lanes)

    def fetch(z, x):
        side_z = 1 - depth_odd if z < HALO else depth_odd
        side_x = 1 - tile_odd if x < HALO else tile_odd
        in_z, in_x = z - HALO, x - HALO
        far_z, far_x = z if z < HALO else in_z - planes, x if x < HALO else in_x - rows
        if 0 <= in_z < planes:
            if 0 <= in_x < rows:
                return own_ref[in_z, in_x]
            return tiles_ref[side_x, in_z, far_x]
        if 0 <= in_x < rows:
            return depths_ref[side_z, far_z, in_x]
        return corners_ref[side_z, side_x, far_z, far_x]

    edge_x, edge_z = edge_list(rows), edge_list(planes)
    for z in edge_z:
        for i in range(0, len(edge_x), 2):
            spots = [(z, edge_x[i]), (z, edge_x[i + 1])]
            sums = conv_spots(taps1_ref, fetch, spots, 1, chans, lanes)
            for (_, x), value in zip(spots, sums):
                hidden_ref[z, x] = silu(value + bias1).astype(BF16)

    @pl.when(tile_index == 0)
    def _():
        hidden_ref[:, 0:2] = jnp.zeros((planes + 4, 2, chans, lanes), BF16)

    @pl.when(tile_index == lax.axis_size("tile") - 1)
    def _():
        hidden_ref[:, rows + 2 :] = jnp.zeros((planes + 4, 2, chans, lanes), BF16)

    @pl.when(depth_index == 0)
    def _():
        hidden_ref[0:2] = jnp.zeros((2, rows + 4, chans, lanes), BF16)

    @pl.when(depth_index == lax.axis_size("depth") - 1)
    def _():
        hidden_ref[planes + 2 :] = jnp.zeros((2, rows + 4, chans, lanes), BF16)

    bias2 = column_of(b2_ref, lanes)
    dens = column_of(dens_ref, lanes)

    def second(pair, carry):
        row = 2 * pair
        image = [jnp.zeros((chans, lanes), F32) for _ in range(2)]
        depth = [jnp.zeros((1, lanes), F32) for _ in range(2)]
        for plane in range(planes):
            sums = conv_spots(
                taps2_ref, lambda z, x: hidden_ref[z, x], [(plane, row), (plane, row + 1)], 2, chans, lanes
            )
            for r in range(2):
                feat = silu(sums[r] + bias2).astype(BF16).astype(F32)
                logit = jnp.sum(feat * dens, axis=0, keepdims=True)
                tau = jax.nn.softplus(logit) * tau_scale
                half = jnp.tanh(0.5 * tau)
                weight = (jnp.exp(-depth[r]) * (2.0 * half / (1.0 + half))).astype(BF16).astype(F32)
                image[r] = image[r] + weight * feat
                depth[r] = depth[r] + tau
        for r in range(2):
            put_image(row + r, rows, image[r], depth[r], depth_odd, unit, send_ref, keep_ref)
        return carry

    lax.fori_loop(0, rows // 2, second, 0)


def merge_rows(rows, mine_ref, other_ref, bit):
    width = mine_ref.shape[1]
    front = bit == 0
    for row in range(rows):
        spot = (rows + row // width, slice(row % width, row % width + 1))
        mine_depth, other_depth = mine_ref[spot], other_ref[spot]
        mine_scale = jnp.where(front, 1.0, jnp.exp(-other_depth))
        other_scale = jnp.where(front, jnp.exp(-mine_depth), 1.0)
        yield row, mine_scale * mine_ref[row] + other_scale * other_ref[row], mine_depth + other_depth


def merge_kernel(rows, level, unit, mine_ref, other_ref, send_ref, keep_ref):
    index = lax.axis_index("depth")
    bit, later = lax.rem(lax.div(index, 1 << level), 2), lax.rem(lax.div(index, 2 << level), 2)
    for row, image, depth in merge_rows(rows, mine_ref, other_ref, bit):
        put_image(row, rows, image, depth, later, unit, send_ref, keep_ref)


def last_kernel(rows, level, mine_ref, other_ref, out_ref):
    bit = lax.rem(lax.div(lax.axis_index("depth"), 1 << level), 2)
    for row, image, _ in merge_rows(rows, mine_ref, other_ref, bit):
        out_ref[:, row] = image


def call(kernel, name, outs, args, flops, limit, aliases=None, scratch=()):
    return pl.pallas_call(
        kernel,
        out_shape=outs,
        in_specs=[VMEM] * len(args),
        out_specs=jax.tree.map(lambda _: VMEM, outs),
        scratch_shapes=scratch,
        input_output_aliases=aliases or {},
        compiler_params=pltpu.CompilerParams(vmem_limit_bytes=limit << 20),
        cost_estimate=pl.CostEstimate(flops=flops, bytes_accessed=1 << 20, transcendentals=0),
        name=name,
    )(*args)


def body(volume, first_kernel, first_bias, second_kernel, second_bias, density_weight):
    chans, planes, rows, lanes = volume.shape
    count = lax.axis_size("depth")
    unit = chans // count
    levels = count.bit_length() - 1
    assert count == 1 << levels and count > 1
    own = volume.transpose(1, 2, 0, 3)
    tiles = jnp.stack(swap_edges(own, "tile", 1, HALO))
    depths = jnp.stack(swap_edges(own, "depth", 0, HALO))
    corners = jnp.stack(swap_edges(tiles, "depth", 1, HALO))
    b1, b2, dens = first_bias[None], second_bias[None], density_weight[None]

    row_flops = 2 * 27 * chans * chans * lanes
    hidden_shape = jax.ShapeDtypeStruct((planes + 4, rows + 4, chans, lanes), BF16)
    taps_shape = jax.ShapeDtypeStruct((3 * chans, 9 * chans), BF16)
    inner, sides = (planes - 2) * (rows - 2), 6 * (planes + rows - 4)
    hidden, taps1, taps2 = call(
        inner_kernel,
        "inner",
        (hidden_shape, taps_shape, taps_shape),
        (own, first_kernel, b1, second_kernel),
        row_flops * inner,
        12,
    )
    hidden = call(
        side_kernel, "sides", hidden_shape, (own, tiles, depths, taps1, b1, hidden), row_flops * sides, 12, {5: 0}
    )

    def image_shape(width):
        return jax.ShapeDtypeStruct((rows + -(-rows // width), width, lanes), F32)

    half = image_shape(chans // 2)
    _, send, keep = call(
        functools.partial(field_kernel, 2.0 / (planes * count), unit),
        "field",
        (hidden_shape, half, half),
        (own, tiles, depths, corners, taps1, b1, taps2, b2, dens, hidden),
        row_flops * (36 + planes * rows),
        12,
        {9: 0},
    )
    for level in range(levels):
        got = lax.ppermute(send, "depth", [(i, i ^ (1 << level)) for i in range(count)])
        if level < levels - 1:
            part = image_shape(send.shape[1] // 2)
            send, keep = call(
                functools.partial(merge_kernel, rows, level, unit), "merge", (part, part), (keep, got), 1 << 20, 4
            )
    return call(
        functools.partial(last_kernel, rows, levels - 1),
        "last",
        jax.ShapeDtypeStruct((unit, rows, lanes), F32),
        (keep, got),
        1 << 20,
        4,
    )


def solution(mesh):
    placed = (P(None, ("groups", "depth"), "tile", None), P(), P(), P(), P(), P())
    return jax.shard_map(
        body,
        mesh=mesh,
        in_specs=placed,
        out_specs=P("depth", ("groups", "tile"), None),
        check_vma=False,
    )
```

```python
import functools

import jax
import jax.numpy as jnp
from jax import lax
from jax.experimental import pallas as pl
from jax.experimental.pallas import tpu as pltpu
from jax.sharding import PartitionSpec as P

BF16 = jnp.bfloat16
F32 = jnp.float32
HALO = 3
VMEM = pl.BlockSpec(memory_space=pltpu.VMEM)


def near_pairs(count):
    return [(i, i ^ 1) for i in range(count) if i ^ 1 < count]


def far_pairs(count):
    lows = [i for i in range(1, count - 1, 2)]
    return [(i, i + 1) for i in lows] + [(i + 1, i) for i in lows]


def partners(axis, far):
    count = lax.axis_size(axis)
    return far_pairs(count) if far else near_pairs(count)


def swap(block, axis, far):
    return lax.ppermute(block, axis, partners(axis, far))


def swap_corner(block, far):
    count = lax.axis_size("depth")
    pairs = [
        (a * count + b, c * count + d) for a, c in partners("tile", far) for b, d in partners("depth", True)
    ]
    return lax.ppermute(block, ("tile", "depth"), pairs)


def spread_kernel(volume_ref, *refs):
    given_refs, (own_ref, tn_ref, tf_ref, dn_ref, df_ref, cn_ref, cf_ref), kept_refs = (
        refs[:5],
        refs[5:12],
        refs[12:17],
    )
    raw_ref, wide_ref, sems, kept_sems = refs[17:]
    planes, rows, chans, lanes = own_ref.shape
    copies = [
        pltpu.make_async_copy(volume_ref.at[:, z], raw_ref.at[z], sems.at[z]) for z in range(planes)
    ]
    others = [
        pltpu.make_async_copy(given, kept, kept_sems.at[i])
        for i, (given, kept) in enumerate(zip(given_refs, kept_refs))
    ]
    for copy in copies + others:
        copy.start()
    for z in range(planes):
        copies[z].wait()
        wide_ref[z % 2] = raw_ref[z].astype(F32).reshape(chans * rows, lanes)
        for x in range(rows):
            own_ref[z, x] = wide_ref[z % 2, pl.ds(x, chans, stride=rows), :].astype(BF16)
    tile_odd, depth_odd = lax.axis_index("tile") % 2, lax.axis_index("depth") % 2
    near_x, far_x = (1 - tile_odd) * (rows - HALO), tile_odd * (rows - HALO)
    near_z, far_z = (1 - depth_odd) * (planes - HALO), depth_odd * (planes - HALO)
    tn_ref[...] = own_ref[:, pl.ds(near_x, HALO)]
    tf_ref[...] = own_ref[:, pl.ds(far_x, HALO)]
    dn_ref[...] = own_ref[pl.ds(near_z, HALO)]
    df_ref[...] = own_ref[pl.ds(far_z, HALO)]
    cn_ref[...] = own_ref[pl.ds(far_z, HALO), pl.ds(near_x, HALO)]
    cf_ref[...] = own_ref[pl.ds(far_z, HALO), pl.ds(far_x, HALO)]
    for copy in others:
        copy.wait()


def cut_kernel(near_ref, far_ref, both_ref, given_ref):
    planes = near_ref.shape[0]
    start = (1 - lax.axis_index("depth") % 2) * (planes - HALO)
    for i, ref in enumerate((near_ref, far_ref)):
        given_ref[i] = ref[pl.ds(start, HALO)]
        both_ref[i] = ref[...]


def shifted_sum(parts, spacing, chans):
    lanes = parts.shape[1]
    column = lax.broadcasted_iota(jnp.int32, (chans, lanes), 1)
    low = pltpu.roll(parts[:chans], spacing, 1)
    high = pltpu.roll(parts[2 * chans :], lanes - spacing, 1)
    return (
        parts[chans : 2 * chans]
        + jnp.where(column >= spacing, low, 0.0)
        + jnp.where(column < lanes - spacing, high, 0.0)
    )


def silu(value):
    half = 0.5 * value
    return half + half * jnp.tanh(half)


def column_of(row_ref, lanes):
    chans = row_ref.shape[1]
    return jnp.broadcast_to(row_ref[...].astype(F32), (lanes, chans)).T


def pack_taps(source_ref, packed_ref):
    chans_out, chans_in = source_ref.shape[1:]
    for tap in range(9):
        packed_ref[:, tap * chans_in : (tap + 1) * chans_in] = source_ref[3 * tap : 3 * tap + 3].reshape(
            3 * chans_out, chans_in
        )


def conv_spots(taps_ref, fetch, spots, spacing, chans, lanes):
    blocks = []
    for dz in range(3):
        for dx in range(3):
            blocks.append(
                jnp.concatenate([fetch(z + spacing * dz, x + spacing * dx) for z, x in spots], axis=1)
            )
    stacked = jnp.concatenate(blocks, axis=0)
    parts = jnp.dot(taps_ref[...], stacked, preferred_element_type=F32)
    return [shifted_sum(parts[:, r * lanes : (r + 1) * lanes], spacing, chans) for r in range(len(spots))]


def edge_list(length):
    return [0, 1, 2, length + 1, length + 2, length + 3]


def inner_kernel(own_ref, w1_ref, b1_ref, w2_ref, hidden_ref, taps1_ref, taps2_ref):
    planes, rows, chans, lanes = own_ref.shape
    pack_taps(w1_ref, taps1_ref)
    bias = column_of(b1_ref, lanes)

    for plane in range(HALO, planes + 1):
        for x in range(HALO, rows + 1, 2):
            spots = [(plane, x), (plane, x + 1)]
            sums = conv_spots(taps1_ref, lambda z, x: own_ref[z - HALO, x - HALO], spots, 1, chans, lanes)
            for (z, x), value in zip(spots, sums):
                hidden_ref[z, x] = silu(value + bias).astype(BF16)
    pack_taps(w2_ref, taps2_ref)


def side_spots(axis, planes, rows):
    if axis == "tile":
        edges = edge_list(rows)
        return [
            [(z, edges[i]), (z, edges[i + 1])] for z in range(HALO, planes + 1) for i in range(0, len(edges), 2)
        ]
    return [[(z, x), (z, x + 1)] for x in range(HALO, rows + 1, 2) for z in edge_list(planes)]


def side_kernel(axis, own_ref, halo_ref, taps_ref, b1_ref, given_ref, hidden_ref):
    planes, rows, chans, lanes = own_ref.shape
    odd = lax.axis_index(axis) % 2
    bias = column_of(b1_ref, lanes)

    def fetch(z, x):
        in_z, in_x = z - HALO, x - HALO
        along, length = (in_x, rows) if axis == "tile" else (in_z, planes)
        if 0 <= along < length:
            return own_ref[in_z, in_x]
        side, far = (1 - odd, along + HALO) if along < 0 else (odd, along - length)
        return halo_ref[side, in_z, far] if axis == "tile" else halo_ref[side, far, in_x]

    for spots in side_spots(axis, planes, rows):
        sums = conv_spots(taps_ref, fetch, spots, 1, chans, lanes)
        for (z, x), value in zip(spots, sums):
            hidden_ref[z, x] = silu(value + bias).astype(BF16)


def split_groups(value, bit, unit):
    groups = [value[i : i + unit] for i in range(0, value.shape[0], unit)]
    even, odd = jnp.concatenate(groups[0::2], axis=0), jnp.concatenate(groups[1::2], axis=0)
    return jnp.where(bit == 1, even, odd), jnp.where(bit == 1, odd, even)


def put_image(row, rows, image, depth, bit, unit, send_ref, keep_ref):
    send, keep = split_groups(image, bit, unit)
    width = send_ref.shape[1]
    for ref, value in ((send_ref, send), (keep_ref, keep)):
        ref[row] = value
        ref[rows + row // width, pl.ds(row % width, 1)] = depth


def field_kernel(
    tau_scale,
    unit,
    own_ref,
    tiles_ref,
    depths_ref,
    corners_ref,
    taps1_ref,
    b1_ref,
    taps2_ref,
    b2_ref,
    dens_ref,
    given_ref,
    hidden_ref,
    send_ref,
    keep_ref,
):
    planes, rows, chans, lanes = own_ref.shape
    tile_index, depth_index = lax.axis_index("tile"), lax.axis_index("depth")
    tile_odd, depth_odd = tile_index % 2, depth_index % 2
    bias1 = column_of(b1_ref, lanes)

    def fetch(z, x):
        side_z = 1 - depth_odd if z < HALO else depth_odd
        side_x = 1 - tile_odd if x < HALO else tile_odd
        in_z, in_x = z - HALO, x - HALO
        far_z, far_x = z if z < HALO else in_z - planes, x if x < HALO else in_x - rows
        if 0 <= in_z < planes:
            if 0 <= in_x < rows:
                return own_ref[in_z, in_x]
            return tiles_ref[side_x, in_z, far_x]
        if 0 <= in_x < rows:
            return depths_ref[side_z, far_z, in_x]
        return corners_ref[side_z, side_x, far_z, far_x]

    edge_x, edge_z = edge_list(rows), edge_list(planes)
    for z in edge_z:
        for i in range(0, len(edge_x), 2):
            spots = [(z, edge_x[i]), (z, edge_x[i + 1])]
            sums = conv_spots(taps1_ref, fetch, spots, 1, chans, lanes)
            for (_, x), value in zip(spots, sums):
                hidden_ref[z, x] = silu(value + bias1).astype(BF16)

    @pl.when(tile_index == 0)
    def _():
        hidden_ref[:, 0:2] = jnp.zeros((planes + 4, 2, chans, lanes), BF16)

    @pl.when(tile_index == lax.axis_size("tile") - 1)
    def _():
        hidden_ref[:, rows + 2 :] = jnp.zeros((planes + 4, 2, chans, lanes), BF16)

    @pl.when(depth_index == 0)
    def _():
        hidden_ref[0:2] = jnp.zeros((2, rows + 4, chans, lanes), BF16)

    @pl.when(depth_index == lax.axis_size("depth") - 1)
    def _():
        hidden_ref[planes + 2 :] = jnp.zeros((2, rows + 4, chans, lanes), BF16)

    bias2 = column_of(b2_ref, lanes)
    dens = column_of(dens_ref, lanes)

    for row in range(0, rows, 2):
        image = [jnp.zeros((chans, lanes), F32) for _ in range(2)]
        depth = [jnp.zeros((1, lanes), F32) for _ in range(2)]
        for plane in range(planes):
            sums = conv_spots(
                taps2_ref, lambda z, x: hidden_ref[z, x], [(plane, row), (plane, row + 1)], 2, chans, lanes
            )
            for r in range(2):
                feat = silu(sums[r] + bias2).astype(BF16).astype(F32)
                logit = jnp.sum(feat * dens, axis=0, keepdims=True)
                tau = jax.nn.softplus(logit) * tau_scale
                half = jnp.tanh(0.5 * tau)
                weight = (jnp.exp(-depth[r]) * (2.0 * half / (1.0 + half))).astype(BF16).astype(F32)
                image[r] = image[r] + weight * feat
                depth[r] = depth[r] + tau
        for r in range(2):
            put_image(row + r, rows, image[r], depth[r], depth_odd, unit, send_ref, keep_ref)


def merge_rows(rows, mine_ref, other_ref, bit):
    width = mine_ref.shape[1]
    front = bit == 0
    for row in range(rows):
        spot = (rows + row // width, slice(row % width, row % width + 1))
        mine_depth, other_depth = mine_ref[spot], other_ref[spot]
        mine_scale = jnp.where(front, 1.0, jnp.exp(-other_depth))
        other_scale = jnp.where(front, jnp.exp(-mine_depth), 1.0)
        yield row, mine_scale * mine_ref[row] + other_scale * other_ref[row], mine_depth + other_depth


def merge_kernel(rows, level, unit, mine_ref, other_ref, send_ref, keep_ref):
    index = lax.axis_index("depth")
    bit, later = lax.rem(lax.div(index, 1 << level), 2), lax.rem(lax.div(index, 2 << level), 2)
    for row, image, depth in merge_rows(rows, mine_ref, other_ref, bit):
        put_image(row, rows, image, depth, later, unit, send_ref, keep_ref)


def last_kernel(rows, level, mine_ref, other_ref, out_ref):
    bit = lax.rem(lax.div(lax.axis_index("depth"), 1 << level), 2)
    for row, image, _ in merge_rows(rows, mine_ref, other_ref, bit):
        out_ref[:, row] = image


def call(kernel, outs, args, flops, limit, aliases=None, scratch=(), space=pltpu.VMEM):
    return pl.pallas_call(
        kernel,
        out_shape=outs,
        in_specs=[pl.BlockSpec(memory_space=space)] * len(args),
        out_specs=jax.tree.map(lambda _: VMEM, outs),
        scratch_shapes=scratch,
        input_output_aliases=aliases or {},
        compiler_params=pltpu.CompilerParams(vmem_limit_bytes=limit << 20),
        cost_estimate=pl.CostEstimate(flops=flops, bytes_accessed=1 << 20, transcendentals=0),
    )(*args)


def body(volume, first_kernel, first_bias, second_kernel, second_bias, density_weight):
    chans, planes, rows, lanes = volume.shape
    count = lax.axis_size("depth")
    unit = chans // count
    levels = count.bit_length() - 1
    assert count == 1 << levels and count > 1

    def field_shape(*dims):
        return jax.ShapeDtypeStruct(dims + (chans, lanes), BF16)

    tile_edge, depth_edge, corner = field_shape(planes, HALO), field_shape(HALO, rows), field_shape(HALO, HALO)
    params = (first_kernel, second_kernel, first_bias[None], second_bias[None], density_weight[None])
    own, tn, tf, dn, df, cn, cf, w1, w2, b1, b2, dens = call(
        spread_kernel,
        (field_shape(planes, rows), tile_edge, tile_edge, depth_edge, depth_edge, corner, corner)
        + tuple(jax.ShapeDtypeStruct(p.shape, p.dtype) for p in params),
        tuple(pltpu.with_memory_space_constraint(p, pltpu.HBM) for p in (volume,) + params),
        1 << 20,
        12,
        scratch=[
            pltpu.VMEM((planes, chans, rows, lanes), BF16),
            pltpu.VMEM((2, chans * rows, lanes), F32),
            pltpu.SemaphoreType.DMA((planes,)),
            pltpu.SemaphoreType.DMA((len(params),)),
        ],
        space=pltpu.HBM,
    )
    tiles, given = call(
        cut_kernel,
        (
            jax.ShapeDtypeStruct((2, planes, HALO, chans, lanes), BF16),
            jax.ShapeDtypeStruct((2, HALO, HALO, chans, lanes), BF16),
        ),
        (swap(tn, "tile", False), swap(tf, "tile", True)),
        1 << 20,
        4,
    )
    far_corners = jnp.stack([swap_corner(cn, False), swap_corner(cf, True)])
    depths = jnp.stack([swap(dn, "depth", False), swap(df, "depth", True)])
    corners = jnp.stack([swap(given, "depth", False), far_corners])

    row_flops = 2 * 27 * chans * chans * lanes
    hidden_shape = jax.ShapeDtypeStruct((planes + 4, rows + 4, chans, lanes), BF16)
    taps_shape = jax.ShapeDtypeStruct((3 * chans, 9 * chans), BF16)
    inner = (planes - 2) * (rows - 2)
    hidden, taps1, taps2 = call(
        inner_kernel, (hidden_shape, taps_shape, taps_shape), (own, w1, b1, w2), row_flops * inner, 12
    )
    for axis, halo, count_rows in (("depth", depths, 6 * (rows - 2)), ("tile", tiles, 6 * (planes - 2))):
        hidden = call(
            functools.partial(side_kernel, axis),
            hidden_shape,
            (own, halo, taps1, b1, hidden),
            row_flops * count_rows,
            12,
            {4: 0},
        )

    def image_shape(width):
        return jax.ShapeDtypeStruct((rows + -(-rows // width), width, lanes), F32)

    half = image_shape(chans // 2)
    _, send, keep = call(
        functools.partial(field_kernel, 2.0 / (planes * count), unit),
        (hidden_shape, half, half),
        (own, tiles, depths, corners, taps1, b1, taps2, b2, dens, hidden),
        row_flops * (36 + planes * rows),
        12,
        {9: 0},
    )
    for level in range(levels):
        got = lax.ppermute(send, "depth", [(i, i ^ (1 << level)) for i in range(count)])
        if level < levels - 1:
            part = image_shape(send.shape[1] // 2)
            send, keep = call(functools.partial(merge_kernel, rows, level, unit), (part, part), (keep, got), 1 << 20, 4)
    return call(
        functools.partial(last_kernel, rows, levels - 1),
        jax.ShapeDtypeStruct((unit, rows, lanes), F32),
        (keep, got),
        1 << 20,
        4,
    )


def solution(mesh):
    placed = (P(None, ("groups", "depth"), "tile", None), P(), P(), P(), P(), P())

    return jax.shard_map(
        body,
        mesh=mesh,
        in_specs=placed,
        out_specs=P("depth", ("groups", "tile"), None),
        check_vma=False,
    )
```

```python
import functools

import jax
import jax.numpy as jnp
from jax import lax
from jax.experimental import pallas as pl
from jax.experimental.pallas import tpu as pltpu
from jax.sharding import PartitionSpec as P

BF16 = jnp.bfloat16
F32 = jnp.float32
HALO = 3
VMEM = pl.BlockSpec(memory_space=pltpu.VMEM)


def near_pairs(count):
    return [(i, i ^ 1) for i in range(count) if i ^ 1 < count]


def far_pairs(count):
    lows = [i for i in range(1, count - 1, 2)]
    return [(i, i + 1) for i in lows] + [(i + 1, i) for i in lows]


def partners(axis, far):
    count = lax.axis_size(axis)
    return far_pairs(count) if far else near_pairs(count)


def swap(block, axis, far):
    return lax.ppermute(block, axis, partners(axis, far))


def swap_corner(block, far):
    count = lax.axis_size("depth")
    pairs = [
        (a * count + b, c * count + d) for a, c in partners("tile", far) for b, d in partners("depth", True)
    ]
    return lax.ppermute(block, ("tile", "depth"), pairs)


def spread_kernel(volume_ref, *refs):
    given_refs, (own_ref, tn_ref, tf_ref, dn_ref, df_ref, cn_ref, cf_ref), kept_refs = (
        refs[:5],
        refs[5:12],
        refs[12:17],
    )
    raw_ref, wide_ref, sems, kept_sems = refs[17:]
    planes, rows, chans, lanes = own_ref.shape
    copies = [
        pltpu.make_async_copy(volume_ref.at[:, z], raw_ref.at[z], sems.at[z]) for z in range(planes)
    ]
    others = [
        pltpu.make_async_copy(given, kept, kept_sems.at[i])
        for i, (given, kept) in enumerate(zip(given_refs, kept_refs))
    ]
    for copy in copies + others:
        copy.start()
    for z in range(planes):
        copies[z].wait()
        wide_ref[z % 2] = raw_ref[z].astype(F32).reshape(chans * rows, lanes)
        for x in range(rows):
            own_ref[z, x] = wide_ref[z % 2, pl.ds(x, chans, stride=rows), :].astype(BF16)
    tile_odd, depth_odd = lax.axis_index("tile") % 2, lax.axis_index("depth") % 2
    near_x, far_x = (1 - tile_odd) * (rows - HALO), tile_odd * (rows - HALO)
    near_z, far_z = (1 - depth_odd) * (planes - HALO), depth_odd * (planes - HALO)
    tn_ref[...] = own_ref[:, pl.ds(near_x, HALO)]
    tf_ref[...] = own_ref[:, pl.ds(far_x, HALO)]
    dn_ref[...] = own_ref[pl.ds(near_z, HALO)]
    df_ref[...] = own_ref[pl.ds(far_z, HALO)]
    cn_ref[...] = own_ref[pl.ds(far_z, HALO), pl.ds(near_x, HALO)]
    cf_ref[...] = own_ref[pl.ds(far_z, HALO), pl.ds(far_x, HALO)]
    for copy in others:
        copy.wait()


def cut_kernel(near_ref, far_ref, both_ref, given_ref):
    planes = near_ref.shape[0]
    start = (1 - lax.axis_index("depth") % 2) * (planes - HALO)
    for i, ref in enumerate((near_ref, far_ref)):
        given_ref[i] = ref[pl.ds(start, HALO)]
        both_ref[i] = ref[...]


def shifted_sum(parts, spacing, chans):
    lanes = parts.shape[1]
    column = lax.broadcasted_iota(jnp.int32, (chans, lanes), 1)
    low = pltpu.roll(parts[:chans], spacing, 1)
    high = pltpu.roll(parts[2 * chans :], lanes - spacing, 1)
    return (
        parts[chans : 2 * chans]
        + jnp.where(column >= spacing, low, 0.0)
        + jnp.where(column < lanes - spacing, high, 0.0)
    )


def silu(value):
    half = 0.5 * value
    return half + half * jnp.tanh(half)


def column_of(row_ref, lanes):
    chans = row_ref.shape[1]
    return jnp.broadcast_to(row_ref[...].astype(F32), (lanes, chans)).T


def pack_taps(source_ref, packed_ref):
    chans_out, chans_in = source_ref.shape[1:]
    for tap in range(9):
        packed_ref[:, tap * chans_in : (tap + 1) * chans_in] = source_ref[3 * tap : 3 * tap + 3].reshape(
            3 * chans_out, chans_in
        )


def conv_spots(taps_ref, fetch, spots, spacing, chans, lanes):
    blocks = []
    for dz in range(3):
        for dx in range(3):
            blocks.append(
                jnp.concatenate([fetch(z + spacing * dz, x + spacing * dx) for z, x in spots], axis=1)
            )
    stacked = jnp.concatenate(blocks, axis=0)
    parts = jnp.dot(taps_ref[...], stacked, preferred_element_type=F32)
    return [shifted_sum(parts[:, r * lanes : (r + 1) * lanes], spacing, chans) for r in range(len(spots))]


def edge_list(length):
    return [0, 1, 2, length + 1, length + 2, length + 3]


def inner_kernel(own_ref, w1_ref, b1_ref, w2_ref, hidden_ref, taps1_ref, taps2_ref):
    planes, rows, chans, lanes = own_ref.shape
    pack_taps(w1_ref, taps1_ref)
    bias = column_of(b1_ref, lanes)

    for plane in range(HALO, planes + 1):
        for x in range(HALO, rows + 1, 2):
            spots = [(plane, x), (plane, x + 1)]
            sums = conv_spots(taps1_ref, lambda z, x: own_ref[z - HALO, x - HALO], spots, 1, chans, lanes)
            for (z, x), value in zip(spots, sums):
                hidden_ref[z, x] = silu(value + bias).astype(BF16)
    pack_taps(w2_ref, taps2_ref)


def side_spots(axis, planes, rows):
    if axis == "tile":
        edges = edge_list(rows)
        return [
            [(z, edges[i]), (z, edges[i + 1])] for z in range(HALO, planes + 1) for i in range(0, len(edges), 2)
        ]
    return [[(z, x), (z, x + 1)] for x in range(HALO, rows + 1, 2) for z in edge_list(planes)]


def depth_kernel(own_ref, halo_ref, taps_ref, b1_ref, given_ref, hidden_ref):
    planes, rows, chans, lanes = own_ref.shape
    put_sides("depth", own_ref, halo_ref, taps_ref, b1_ref, hidden_ref)
    index = lax.axis_index("depth")
    inside = rows - 2

    @pl.when(index == 0)
    def _():
        hidden_ref[0:2, HALO : rows + 1] = jnp.zeros((2, inside, chans, lanes), BF16)

    @pl.when(index == lax.axis_size("depth") - 1)
    def _():
        hidden_ref[planes + 2 :, HALO : rows + 1] = jnp.zeros((2, inside, chans, lanes), BF16)


def tile_kernel(
    tau_scale,
    own_ref,
    halo_ref,
    taps1_ref,
    b1_ref,
    taps2_ref,
    b2_ref,
    dens_ref,
    given_ref,
    hidden_ref,
    middle_ref,
):
    planes, rows, chans, _ = own_ref.shape
    put_sides("tile", own_ref, halo_ref, taps1_ref, b1_ref, hidden_ref)
    pieces = render(tau_scale, planes, middle_rows(rows), taps2_ref, b2_ref, dens_ref, hidden_ref)
    for at, (_, image, depth) in enumerate(pieces):
        middle_ref[at, :chans] = image
        middle_ref[at, chans : chans + 1] = depth


def put_sides(axis, own_ref, halo_ref, taps_ref, b1_ref, hidden_ref):
    planes, rows, chans, lanes = own_ref.shape
    odd = lax.axis_index(axis) % 2
    bias = column_of(b1_ref, lanes)

    def fetch(z, x):
        in_z, in_x = z - HALO, x - HALO
        along, length = (in_x, rows) if axis == "tile" else (in_z, planes)
        if 0 <= along < length:
            return own_ref[in_z, in_x]
        side, far = (1 - odd, along + HALO) if along < 0 else (odd, along - length)
        return halo_ref[side, in_z, far] if axis == "tile" else halo_ref[side, far, in_x]

    for spots in side_spots(axis, planes, rows):
        sums = conv_spots(taps_ref, fetch, spots, 1, chans, lanes)
        for (z, x), value in zip(spots, sums):
            hidden_ref[z, x] = silu(value + bias).astype(BF16)


def split_groups(value, bit, unit):
    groups = [value[i : i + unit] for i in range(0, value.shape[0], unit)]
    even, odd = jnp.concatenate(groups[0::2], axis=0), jnp.concatenate(groups[1::2], axis=0)
    return jnp.where(bit == 1, even, odd), jnp.where(bit == 1, odd, even)


def put_image(row, rows, image, depth, bit, unit, send_ref, keep_ref):
    send, keep = split_groups(image, bit, unit)
    width = send_ref.shape[1]
    for ref, value in ((send_ref, send), (keep_ref, keep)):
        ref[row] = value
        ref[rows + row // width, pl.ds(row % width, 1)] = depth


def middle_rows(rows):
    return list(range(HALO, rows - HALO))


def render(tau_scale, planes, rows, taps_ref, b2_ref, dens_ref, hidden_ref):
    chans, lanes = hidden_ref.shape[2:]
    bias, dens = column_of(b2_ref, lanes), column_of(dens_ref, lanes)
    for start in range(0, len(rows), 2):
        pair = rows[start : start + 2]
        image = [jnp.zeros((chans, lanes), F32) for _ in pair]
        depth = [jnp.zeros((1, lanes), F32) for _ in pair]
        for plane in range(planes):
            spots = [(plane, row) for row in pair]
            sums = conv_spots(taps_ref, lambda z, x: hidden_ref[z, x], spots, 2, chans, lanes)
            for r, value in enumerate(sums):
                feat = silu(value + bias).astype(BF16).astype(F32)
                logit = jnp.sum(feat * dens, axis=0, keepdims=True)
                tau = jax.nn.softplus(logit) * tau_scale
                half = jnp.tanh(0.5 * tau)
                weight = (jnp.exp(-depth[r]) * (2.0 * half / (1.0 + half))).astype(BF16).astype(F32)
                image[r] = image[r] + weight * feat
                depth[r] = depth[r] + tau
        yield from zip(pair, image, depth)


def field_kernel(
    tau_scale,
    unit,
    own_ref,
    tiles_ref,
    depths_ref,
    corners_ref,
    taps1_ref,
    b1_ref,
    taps2_ref,
    b2_ref,
    dens_ref,
    given_ref,
    middle_ref,
    hidden_ref,
    send_ref,
    keep_ref,
):
    planes, rows, chans, lanes = own_ref.shape
    tile_index, depth_index = lax.axis_index("tile"), lax.axis_index("depth")
    tile_odd, depth_odd = tile_index % 2, depth_index % 2
    bias1 = column_of(b1_ref, lanes)

    def fetch(z, x):
        side_z = 1 - depth_odd if z < HALO else depth_odd
        side_x = 1 - tile_odd if x < HALO else tile_odd
        in_z, in_x = z - HALO, x - HALO
        far_z, far_x = z if z < HALO else in_z - planes, x if x < HALO else in_x - rows
        if 0 <= in_z < planes:
            if 0 <= in_x < rows:
                return own_ref[in_z, in_x]
            return tiles_ref[side_x, in_z, far_x]
        if 0 <= in_x < rows:
            return depths_ref[side_z, far_z, in_x]
        return corners_ref[side_z, side_x, far_z, far_x]

    edge_x, edge_z = edge_list(rows), edge_list(planes)
    for z in edge_z:
        for i in range(0, len(edge_x), 2):
            spots = [(z, edge_x[i]), (z, edge_x[i + 1])]
            sums = conv_spots(taps1_ref, fetch, spots, 1, chans, lanes)
            for (_, x), value in zip(spots, sums):
                hidden_ref[z, x] = silu(value + bias1).astype(BF16)

    @pl.when(tile_index == 0)
    def _():
        hidden_ref[:, 0:2] = jnp.zeros((planes + 4, 2, chans, lanes), BF16)

    @pl.when(tile_index == lax.axis_size("tile") - 1)
    def _():
        hidden_ref[:, rows + 2 :] = jnp.zeros((planes + 4, 2, chans, lanes), BF16)

    @pl.when(depth_index == 0)
    def _():
        hidden_ref[0:2] = jnp.zeros((2, rows + 4, chans, lanes), BF16)

    @pl.when(depth_index == lax.axis_size("depth") - 1)
    def _():
        hidden_ref[planes + 2 :] = jnp.zeros((2, rows + 4, chans, lanes), BF16)

    for at, row in enumerate(middle_rows(rows)):
        put_image(row, rows, middle_ref[at, :chans], middle_ref[at, chans : chans + 1], depth_odd, unit, send_ref, keep_ref)
    outer = [row for row in range(rows) if row not in middle_rows(rows)]
    for row, image, depth in render(tau_scale, planes, outer, taps2_ref, b2_ref, dens_ref, hidden_ref):
        put_image(row, rows, image, depth, depth_odd, unit, send_ref, keep_ref)


def merge_rows(rows, mine_ref, other_ref, bit):
    width = mine_ref.shape[1]
    front = bit == 0
    for row in range(rows):
        spot = (rows + row // width, slice(row % width, row % width + 1))
        mine_depth, other_depth = mine_ref[spot], other_ref[spot]
        mine_scale = jnp.where(front, 1.0, jnp.exp(-other_depth))
        other_scale = jnp.where(front, jnp.exp(-mine_depth), 1.0)
        yield row, mine_scale * mine_ref[row] + other_scale * other_ref[row], mine_depth + other_depth


def merge_kernel(rows, level, unit, mine_ref, other_ref, send_ref, keep_ref):
    index = lax.axis_index("depth")
    bit, later = lax.rem(lax.div(index, 1 << level), 2), lax.rem(lax.div(index, 2 << level), 2)
    for row, image, depth in merge_rows(rows, mine_ref, other_ref, bit):
        put_image(row, rows, image, depth, later, unit, send_ref, keep_ref)


def last_kernel(rows, level, mine_ref, other_ref, out_ref):
    bit = lax.rem(lax.div(lax.axis_index("depth"), 1 << level), 2)
    for row, image, _ in merge_rows(rows, mine_ref, other_ref, bit):
        out_ref[:, row] = image


def call(kernel, outs, args, flops, limit, aliases=None, scratch=(), space=pltpu.VMEM):
    return pl.pallas_call(
        kernel,
        out_shape=outs,
        in_specs=[pl.BlockSpec(memory_space=space)] * len(args),
        out_specs=jax.tree.map(lambda _: VMEM, outs),
        scratch_shapes=scratch,
        input_output_aliases=aliases or {},
        compiler_params=pltpu.CompilerParams(vmem_limit_bytes=limit << 20),
        cost_estimate=pl.CostEstimate(flops=flops, bytes_accessed=1 << 20, transcendentals=0),
    )(*args)


def body(volume, first_kernel, first_bias, second_kernel, second_bias, density_weight):
    chans, planes, rows, lanes = volume.shape
    count = lax.axis_size("depth")
    unit = chans // count
    levels = count.bit_length() - 1
    assert count == 1 << levels and count > 1

    def field_shape(*dims):
        return jax.ShapeDtypeStruct(dims + (chans, lanes), BF16)

    tile_edge, depth_edge, corner = field_shape(planes, HALO), field_shape(HALO, rows), field_shape(HALO, HALO)
    params = (first_kernel, second_kernel, first_bias[None], second_bias[None], density_weight[None])
    own, tn, tf, dn, df, cn, cf, w1, w2, b1, b2, dens = call(
        spread_kernel,
        (field_shape(planes, rows), tile_edge, tile_edge, depth_edge, depth_edge, corner, corner)
        + tuple(jax.ShapeDtypeStruct(p.shape, p.dtype) for p in params),
        tuple(pltpu.with_memory_space_constraint(p, pltpu.HBM) for p in (volume,) + params),
        1 << 20,
        12,
        scratch=[
            pltpu.VMEM((planes, chans, rows, lanes), BF16),
            pltpu.VMEM((2, chans * rows, lanes), F32),
            pltpu.SemaphoreType.DMA((planes,)),
            pltpu.SemaphoreType.DMA((len(params),)),
        ],
        space=pltpu.HBM,
    )
    tiles, given = call(
        cut_kernel,
        (
            jax.ShapeDtypeStruct((2, planes, HALO, chans, lanes), BF16),
            jax.ShapeDtypeStruct((2, HALO, HALO, chans, lanes), BF16),
        ),
        (swap(tn, "tile", False), swap(tf, "tile", True)),
        1 << 20,
        4,
    )
    far_corners = jnp.stack([swap_corner(cn, False), swap_corner(cf, True)])
    depths = jnp.stack([swap(dn, "depth", False), swap(df, "depth", True)])
    corners = jnp.stack([swap(given, "depth", False), far_corners])

    row_flops = 2 * 27 * chans * chans * lanes
    hidden_shape = jax.ShapeDtypeStruct((planes + 4, rows + 4, chans, lanes), BF16)
    taps_shape = jax.ShapeDtypeStruct((3 * chans, 9 * chans), BF16)
    inner = (planes - 2) * (rows - 2)
    hidden, taps1, taps2 = call(
        inner_kernel, (hidden_shape, taps_shape, taps_shape), (own, w1, b1, w2), row_flops * inner, 12
    )
    tau_scale = 2.0 / (planes * count)
    hidden = call(depth_kernel, hidden_shape, (own, depths, taps1, b1, hidden), row_flops * 6 * (rows - 2), 12, {4: 0})
    mids = len(middle_rows(rows))
    hidden, middle = call(
        functools.partial(tile_kernel, tau_scale),
        (hidden_shape, jax.ShapeDtypeStruct((mids, chans + 8, lanes), F32)),
        (own, tiles, taps1, b1, taps2, b2, dens, hidden),
        row_flops * (6 * (planes - 2) + mids * planes),
        12,
        {7: 0},
    )

    def image_shape(width):
        return jax.ShapeDtypeStruct((rows + -(-rows // width), width, lanes), F32)

    half = image_shape(chans // 2)
    _, send, keep = call(
        functools.partial(field_kernel, tau_scale, unit),
        (hidden_shape, half, half),
        (own, tiles, depths, corners, taps1, b1, taps2, b2, dens, hidden, middle),
        row_flops * (36 + planes * (rows - mids)),
        12,
        {9: 0},
    )
    for level in range(levels):
        got = lax.ppermute(send, "depth", [(i, i ^ (1 << level)) for i in range(count)])
        if level < levels - 1:
            part = image_shape(send.shape[1] // 2)
            send, keep = call(functools.partial(merge_kernel, rows, level, unit), (part, part), (keep, got), 1 << 20, 4)
    return call(
        functools.partial(last_kernel, rows, levels - 1),
        jax.ShapeDtypeStruct((unit, rows, lanes), F32),
        (keep, got),
        1 << 20,
        4,
    )


def solution(mesh):
    placed = (P(None, ("groups", "depth"), "tile", None), P(), P(), P(), P(), P())

    return jax.shard_map(
        body,
        mesh=mesh,
        in_specs=placed,
        out_specs=P("depth", ("groups", "tile"), None),
        check_vma=False,
    )
```

```python
import functools

import jax
import jax.numpy as jnp
from jax import lax
from jax.experimental import pallas as pl
from jax.experimental.pallas import tpu as pltpu
from jax.sharding import PartitionSpec as P

BF16 = jnp.bfloat16
F32 = jnp.float32
HALO = 3
VMEM = pl.BlockSpec(memory_space=pltpu.VMEM)


def near_pairs(count):
    return [(i, i ^ 1) for i in range(count) if i ^ 1 < count]


def far_pairs(count):
    lows = [i for i in range(1, count - 1, 2)]
    return [(i, i + 1) for i in lows] + [(i + 1, i) for i in lows]


def partners(axis, far):
    count = lax.axis_size(axis)
    return far_pairs(count) if far else near_pairs(count)


def swap(block, axis, far, name):
    pairs = partners(axis, far)
    if name == "tile_far":
        pairs = pairs + [(i, i) for i in sorted({0, lax.axis_size(axis) - 1})]
    return lax.ppermute(block, axis, pairs)


def swap_corner(block, far):
    count = lax.axis_size("depth")
    pairs = [
        (a * count + b, c * count + d) for a, c in partners("tile", far) for b, d in partners("depth", True)
    ]
    return lax.ppermute(block, ("tile", "depth"), pairs)


def spread_kernel(volume_ref, *refs):
    given_refs, (own_ref, tn_ref, tf_ref, dn_ref, df_ref, cn_ref, cf_ref), kept_refs = (
        refs[:5],
        refs[5:12],
        refs[12:17],
    )
    raw_ref, wide_ref, sems, kept_sems = refs[17:]
    planes, rows, chans, lanes = own_ref.shape
    copies = [
        pltpu.make_async_copy(volume_ref.at[:, z], raw_ref.at[z], sems.at[z]) for z in range(planes)
    ]
    others = [
        pltpu.make_async_copy(given, kept, kept_sems.at[i])
        for i, (given, kept) in enumerate(zip(given_refs, kept_refs))
    ]
    for copy in copies + others:
        copy.start()
    for z in range(planes):
        copies[z].wait()
        wide_ref[z % 2] = raw_ref[z].astype(F32).reshape(chans * rows, lanes)
        for x in range(rows):
            own_ref[z, x] = wide_ref[z % 2, pl.ds(x, chans, stride=rows), :].astype(BF16)
    tile_odd, depth_odd = lax.axis_index("tile") % 2, lax.axis_index("depth") % 2
    near_x, far_x = (1 - tile_odd) * (rows - HALO), tile_odd * (rows - HALO)
    near_z, far_z = (1 - depth_odd) * (planes - HALO), depth_odd * (planes - HALO)
    tn_ref[...] = own_ref[:, pl.ds(near_x, HALO)]
    tf_ref[...] = own_ref[:, pl.ds(far_x, HALO)]
    dn_ref[...] = own_ref[pl.ds(near_z, HALO)]
    df_ref[...] = own_ref[pl.ds(far_z, HALO)]
    cn_ref[...] = own_ref[pl.ds(far_z, HALO), pl.ds(near_x, HALO)]
    cf_ref[...] = own_ref[pl.ds(far_z, HALO), pl.ds(far_x, HALO)]
    for copy in others:
        copy.wait()


def cut_kernel(near_ref, far_ref, both_ref, given_ref):
    planes = near_ref.shape[0]
    start = (1 - lax.axis_index("depth") % 2) * (planes - HALO)
    for i, ref in enumerate((near_ref, far_ref)):
        given_ref[i] = ref[pl.ds(start, HALO)]
        both_ref[i] = ref[...]
    index = lax.axis_index("tile")

    @pl.when((index == 0) | (index == lax.axis_size("tile") - 1))
    def _():
        both_ref[1] = jnp.zeros(both_ref.shape[1:], BF16)
        given_ref[1] = jnp.zeros(given_ref.shape[1:], BF16)


def shifted_sum(parts, spacing, chans):
    lanes = parts.shape[1]
    column = lax.broadcasted_iota(jnp.int32, (chans, lanes), 1)
    low = pltpu.roll(parts[:chans], spacing, 1)
    high = pltpu.roll(parts[2 * chans :], lanes - spacing, 1)
    return (
        parts[chans : 2 * chans]
        + jnp.where(column >= spacing, low, 0.0)
        + jnp.where(column < lanes - spacing, high, 0.0)
    )


def silu(value):
    half = 0.5 * value
    return half + half * jnp.tanh(half)


def column_of(row_ref, lanes):
    chans = row_ref.shape[1]
    return jnp.broadcast_to(row_ref[...].astype(F32), (lanes, chans)).T


def pack_taps(source_ref, packed_ref):
    chans_out, chans_in = source_ref.shape[1:]
    for tap in range(9):
        packed_ref[:, tap * chans_in : (tap + 1) * chans_in] = source_ref[3 * tap : 3 * tap + 3].reshape(
            3 * chans_out, chans_in
        )


def conv_spots(taps_ref, fetch, spots, spacing, chans, lanes):
    blocks = []
    for dz in range(3):
        for dx in range(3):
            blocks.append(
                jnp.concatenate([fetch(z + spacing * dz, x + spacing * dx) for z, x in spots], axis=1)
            )
    stacked = jnp.concatenate(blocks, axis=0)
    parts = jnp.dot(taps_ref[...], stacked, preferred_element_type=F32)
    return [shifted_sum(parts[:, r * lanes : (r + 1) * lanes], spacing, chans) for r in range(len(spots))]


def edge_list(length):
    return [0, 1, 2, length + 1, length + 2, length + 3]


def inner_kernel(own_ref, w1_ref, b1_ref, w2_ref, hidden_ref, taps1_ref, taps2_ref):
    planes, rows, chans, lanes = own_ref.shape
    pack_taps(w1_ref, taps1_ref)
    bias = column_of(b1_ref, lanes)

    for plane in range(HALO, planes + 1):
        for x in range(HALO, rows + 1, 2):
            spots = [(plane, x), (plane, x + 1)]
            sums = conv_spots(taps1_ref, lambda z, x: own_ref[z - HALO, x - HALO], spots, 1, chans, lanes)
            for (z, x), value in zip(spots, sums):
                hidden_ref[z, x] = silu(value + bias).astype(BF16)
    pack_taps(w2_ref, taps2_ref)


def side_spots(axis, planes, rows):
    if axis == "tile":
        edges = edge_list(rows)
        return [
            [(z, edges[i]), (z, edges[i + 1])] for z in range(HALO, planes + 1) for i in range(0, len(edges), 2)
        ]
    return [[(z, x), (z, x + 1)] for x in range(HALO, rows + 1, 2) for z in edge_list(planes)]


def depth_kernel(own_ref, halo_ref, taps_ref, b1_ref, given_ref, hidden_ref):
    planes, rows, chans, lanes = own_ref.shape
    put_sides("depth", own_ref, halo_ref, taps_ref, b1_ref, hidden_ref)
    index = lax.axis_index("depth")
    inside = rows - 2

    @pl.when(index == 0)
    def _():
        hidden_ref[0:2, HALO : rows + 1] = jnp.zeros((2, inside, chans, lanes), BF16)

    @pl.when(index == lax.axis_size("depth") - 1)
    def _():
        hidden_ref[planes + 2 :, HALO : rows + 1] = jnp.zeros((2, inside, chans, lanes), BF16)


def tile_kernel(
    tau_scale,
    own_ref,
    halo_ref,
    taps1_ref,
    b1_ref,
    taps2_ref,
    b2_ref,
    dens_ref,
    given_ref,
    hidden_ref,
    middle_ref,
):
    planes, rows, chans, _ = own_ref.shape
    put_sides("tile", own_ref, halo_ref, taps1_ref, b1_ref, hidden_ref)
    pieces = render(tau_scale, planes, middle_rows(rows), taps2_ref, b2_ref, dens_ref, hidden_ref)
    for at, (_, image, depth) in enumerate(pieces):
        middle_ref[at, :chans] = image
        middle_ref[at, chans : chans + 1] = depth


def put_sides(axis, own_ref, halo_ref, taps_ref, b1_ref, hidden_ref):
    planes, rows, chans, lanes = own_ref.shape
    odd = lax.axis_index(axis) % 2
    bias = column_of(b1_ref, lanes)

    def fetch(z, x):
        in_z, in_x = z - HALO, x - HALO
        along, length = (in_x, rows) if axis == "tile" else (in_z, planes)
        if 0 <= along < length:
            return own_ref[in_z, in_x]
        side, far = (1 - odd, along + HALO) if along < 0 else (odd, along - length)
        return halo_ref[side, in_z, far] if axis == "tile" else halo_ref[side, far, in_x]

    for spots in side_spots(axis, planes, rows):
        sums = conv_spots(taps_ref, fetch, spots, 1, chans, lanes)
        for (z, x), value in zip(spots, sums):
            hidden_ref[z, x] = silu(value + bias).astype(BF16)


def split_groups(value, bit, unit):
    groups = [value[i : i + unit] for i in range(0, value.shape[0], unit)]
    even, odd = jnp.concatenate(groups[0::2], axis=0), jnp.concatenate(groups[1::2], axis=0)
    return jnp.where(bit == 1, even, odd), jnp.where(bit == 1, odd, even)


def put_image(row, rows, image, depth, bit, unit, send_ref, keep_ref):
    send, keep = split_groups(image, bit, unit)
    width = send_ref.shape[1]
    for ref, value in ((send_ref, send), (keep_ref, keep)):
        ref[row] = value
        ref[rows + row // width, pl.ds(row % width, 1)] = depth


def middle_rows(rows):
    return list(range(HALO, rows - HALO))


def render(tau_scale, planes, rows, taps_ref, b2_ref, dens_ref, hidden_ref):
    chans, lanes = hidden_ref.shape[2:]
    bias, dens = column_of(b2_ref, lanes), column_of(dens_ref, lanes)
    for start in range(0, len(rows), 2):
        pair = rows[start : start + 2]
        image = [jnp.zeros((chans, lanes), F32) for _ in pair]
        depth = [jnp.zeros((1, lanes), F32) for _ in pair]
        for plane in range(planes):
            spots = [(plane, row) for row in pair]
            sums = conv_spots(taps_ref, lambda z, x: hidden_ref[z, x], spots, 2, chans, lanes)
            for r, value in enumerate(sums):
                feat = silu(value + bias).astype(BF16).astype(F32)
                logit = jnp.sum(feat * dens, axis=0, keepdims=True)
                tau = jax.nn.softplus(logit) * tau_scale
                half = jnp.tanh(0.5 * tau)
                weight = (jnp.exp(-depth[r]) * (2.0 * half / (1.0 + half))).astype(BF16).astype(F32)
                image[r] = image[r] + weight * feat
                depth[r] = depth[r] + tau
        yield from zip(pair, image, depth)


def field_kernel(
    tau_scale,
    unit,
    own_ref,
    tiles_ref,
    depths_ref,
    corners_ref,
    taps1_ref,
    b1_ref,
    taps2_ref,
    b2_ref,
    dens_ref,
    given_ref,
    middle_ref,
    hidden_ref,
    send_ref,
    keep_ref,
):
    planes, rows, chans, lanes = own_ref.shape
    tile_index, depth_index = lax.axis_index("tile"), lax.axis_index("depth")
    tile_odd, depth_odd = tile_index % 2, depth_index % 2
    bias1 = column_of(b1_ref, lanes)

    def fetch(z, x):
        side_z = 1 - depth_odd if z < HALO else depth_odd
        side_x = 1 - tile_odd if x < HALO else tile_odd
        in_z, in_x = z - HALO, x - HALO
        far_z, far_x = z if z < HALO else in_z - planes, x if x < HALO else in_x - rows
        if 0 <= in_z < planes:
            if 0 <= in_x < rows:
                return own_ref[in_z, in_x]
            return tiles_ref[side_x, in_z, far_x]
        if 0 <= in_x < rows:
            return depths_ref[side_z, far_z, in_x]
        return corners_ref[side_z, side_x, far_z, far_x]

    edge_x, edge_z = edge_list(rows), edge_list(planes)
    for z in edge_z:
        for i in range(0, len(edge_x), 2):
            spots = [(z, edge_x[i]), (z, edge_x[i + 1])]
            sums = conv_spots(taps1_ref, fetch, spots, 1, chans, lanes)
            for (_, x), value in zip(spots, sums):
                hidden_ref[z, x] = silu(value + bias1).astype(BF16)

    @pl.when(tile_index == 0)
    def _():
        hidden_ref[:, 0:2] = jnp.zeros((planes + 4, 2, chans, lanes), BF16)

    @pl.when(tile_index == lax.axis_size("tile") - 1)
    def _():
        hidden_ref[:, rows + 2 :] = jnp.zeros((planes + 4, 2, chans, lanes), BF16)

    @pl.when(depth_index == 0)
    def _():
        hidden_ref[0:2] = jnp.zeros((2, rows + 4, chans, lanes), BF16)

    @pl.when(depth_index == lax.axis_size("depth") - 1)
    def _():
        hidden_ref[planes + 2 :] = jnp.zeros((2, rows + 4, chans, lanes), BF16)

    for at, row in enumerate(middle_rows(rows)):
        put_image(row, rows, middle_ref[at, :chans], middle_ref[at, chans : chans + 1], depth_odd, unit, send_ref, keep_ref)
    outer = [row for row in range(rows) if row not in middle_rows(rows)]
    for row, image, depth in render(tau_scale, planes, outer, taps2_ref, b2_ref, dens_ref, hidden_ref):
        put_image(row, rows, image, depth, depth_odd, unit, send_ref, keep_ref)


def merge_rows(rows, mine_ref, other_ref, bit):
    width = mine_ref.shape[1]
    front = bit == 0
    for row in range(rows):
        spot = (rows + row // width, slice(row % width, row % width + 1))
        mine_depth, other_depth = mine_ref[spot], other_ref[spot]
        mine_scale = jnp.where(front, 1.0, jnp.exp(-other_depth))
        other_scale = jnp.where(front, jnp.exp(-mine_depth), 1.0)
        yield row, mine_scale * mine_ref[row] + other_scale * other_ref[row], mine_depth + other_depth


def merge_kernel(rows, level, unit, mine_ref, other_ref, send_ref, keep_ref):
    index = lax.axis_index("depth")
    bit, later = lax.rem(lax.div(index, 1 << level), 2), lax.rem(lax.div(index, 2 << level), 2)
    for row, image, depth in merge_rows(rows, mine_ref, other_ref, bit):
        put_image(row, rows, image, depth, later, unit, send_ref, keep_ref)


def last_kernel(rows, level, mine_ref, other_ref, out_ref):
    bit = lax.rem(lax.div(lax.axis_index("depth"), 1 << level), 2)
    for row, image, _ in merge_rows(rows, mine_ref, other_ref, bit):
        out_ref[:, row] = image


def call(kernel, outs, args, flops, limit, aliases=None, scratch=(), space=pltpu.VMEM):
    return pl.pallas_call(
        kernel,
        out_shape=outs,
        in_specs=[pl.BlockSpec(memory_space=space)] * len(args),
        out_specs=jax.tree.map(lambda _: VMEM, outs),
        scratch_shapes=scratch,
        input_output_aliases=aliases or {},
        compiler_params=pltpu.CompilerParams(vmem_limit_bytes=limit << 20),
        cost_estimate=pl.CostEstimate(flops=flops, bytes_accessed=1 << 20, transcendentals=0),
    )(*args)


def body(volume, first_kernel, first_bias, second_kernel, second_bias, density_weight):
    chans, planes, rows, lanes = volume.shape
    count = lax.axis_size("depth")
    unit = chans // count
    levels = count.bit_length() - 1
    assert count == 1 << levels and count > 1

    def field_shape(*dims):
        return jax.ShapeDtypeStruct(dims + (chans, lanes), BF16)

    tile_edge, depth_edge, corner = field_shape(planes, HALO), field_shape(HALO, rows), field_shape(HALO, HALO)
    params = (first_kernel, second_kernel, first_bias[None], second_bias[None], density_weight[None])
    own, tn, tf, dn, df, cn, cf, w1, w2, b1, b2, dens = call(
        spread_kernel,
        (field_shape(planes, rows), tile_edge, tile_edge, depth_edge, depth_edge, corner, corner)
        + tuple(jax.ShapeDtypeStruct(p.shape, p.dtype) for p in params),
        tuple(pltpu.with_memory_space_constraint(p, pltpu.HBM) for p in (volume,) + params),
        1 << 20,
        12,
        scratch=[
            pltpu.VMEM((planes, chans, rows, lanes), BF16),
            pltpu.VMEM((2, chans * rows, lanes), F32),
            pltpu.SemaphoreType.DMA((planes,)),
            pltpu.SemaphoreType.DMA((len(params),)),
        ],
        space=pltpu.HBM,
    )
    tiles, given = call(
        cut_kernel,
        (
            jax.ShapeDtypeStruct((2, planes, HALO, chans, lanes), BF16),
            jax.ShapeDtypeStruct((2, HALO, HALO, chans, lanes), BF16),
        ),
        (swap(tn, "tile", False, "tile_near"), swap(tf, "tile", True, "tile_far")),
        1 << 20,
        4,
    )
    far_corners = jnp.stack([swap_corner(cn, False), swap_corner(cf, True)])
    depths = jnp.stack([swap(dn, "depth", False, "depth_near"), swap(df, "depth", True, "depth_far")])
    corners = jnp.stack([swap(given, "depth", False, "forward"), far_corners])

    row_flops = 2 * 27 * chans * chans * lanes
    hidden_shape = jax.ShapeDtypeStruct((planes + 4, rows + 4, chans, lanes), BF16)
    taps_shape = jax.ShapeDtypeStruct((3 * chans, 9 * chans), BF16)
    inner = (planes - 2) * (rows - 2)
    hidden, taps1, taps2 = call(
        inner_kernel, (hidden_shape, taps_shape, taps_shape), (own, w1, b1, w2), row_flops * inner, 12
    )
    tau_scale = 2.0 / (planes * count)
    hidden = call(depth_kernel, hidden_shape, (own, depths, taps1, b1, hidden), row_flops * 6 * (rows - 2), 12, {4: 0})
    mids = len(middle_rows(rows))
    hidden, middle = call(
        functools.partial(tile_kernel, tau_scale),
        (hidden_shape, jax.ShapeDtypeStruct((mids, chans + 8, lanes), F32)),
        (own, tiles, taps1, b1, taps2, b2, dens, hidden),
        row_flops * (6 * (planes - 2) + mids * planes),
        12,
        {7: 0},
    )

    def image_shape(width):
        return jax.ShapeDtypeStruct((rows + -(-rows // width), width, lanes), F32)

    half = image_shape(chans // 2)
    _, send, keep = call(
        functools.partial(field_kernel, tau_scale, unit),
        (hidden_shape, half, half),
        (own, tiles, depths, corners, taps1, b1, taps2, b2, dens, hidden, middle),
        row_flops * (36 + planes * (rows - mids)),
        12,
        {9: 0},
    )
    for level in range(levels):
        got = lax.ppermute(send, "depth", [(i, i ^ (1 << level)) for i in range(count)])
        if level < levels - 1:
            part = image_shape(send.shape[1] // 2)
            send, keep = call(functools.partial(merge_kernel, rows, level, unit), (part, part), (keep, got), 1 << 20, 4)
    return call(
        functools.partial(last_kernel, rows, levels - 1),
        jax.ShapeDtypeStruct((unit, rows, lanes), F32),
        (keep, got),
        1 << 20,
        4,
    )


def solution(mesh):
    placed = (P(None, ("groups", "depth"), "tile", None), P(), P(), P(), P(), P())

    return jax.shard_map(
        body,
        mesh=mesh,
        in_specs=placed,
        out_specs=P("depth", ("groups", "tile"), None),
        check_vma=False,
    )
```
